32 devices in a mesh: site: 32 (over z, y, x, core).
Axes of the slice: x: 2, y: 2, z: 4, core: 2. Of those that a mesh axis runs over, the one named last changes fastest.
Arguments:
- sites: float32 [32, 2, 12, 128, 128], P('site'), may hold values from -0.5 to 0.5
- sector_sizes: int32 [32, 12], P('site'), may hold values from 64 to 128, as said below
- charge_steps: int32 [32], P('site'), may hold values from 0 to 1
- kept_counts: int32 [32, 12], P('site'), may hold values from 64 to 128, as said below
- gates: float32 [32, 6], P('site'), may hold values from 0.4 to 1.2
- sketches: float32 [32, 12, 256, 128], P('site'), may hold values from -0.375 to 0.375
Outputs:
- new_sites: float32 [32, 2, 12, 128, 128], P('site')
- totals: float32 [2], replicated
The draws below stay inside these ranges and needn't reach their ends.
Inputs may be any that keep to these rules, and one draw needn't show every extreme that they name: `sector_sizes`: every sector holds at least 64 states; each bond has one sector of exactly 128 states. kept_counts[i, c] is at least 64 and at most sector_sizes[(i + 1) mod 32, c]; on each bond the sector of 128 states keeps all of them.
All inputs are finite; a program needn't handle non-finite values.
Results may differ from the reference program's by a relative error of at most 0.0003.
Values sent between devices are 32-bit elements; how exact they have to be, the bound alone decides.
A program may use at most 64 MiB of HBM per device.

```python
import jax
import jax.numpy as jnp
from jax import lax

NSEC = 12
SMAX = 128
STEPS = 4
SITES = 32


def label_tables(key):
    sizes = jax.random.randint(jax.random.fold_in(key, 101), (SITES, NSEC), SMAX // 2, SMAX + 1)
    full_at = jax.random.randint(jax.random.fold_in(key, 102), (SITES,), 0, NSEC)
    sectors = jnp.arange(NSEC)[None, :]
    sizes = jnp.where(sectors == full_at[:, None], SMAX, sizes)
    following = jnp.roll(sizes, -1, axis=0)
    kept = jax.random.randint(jax.random.fold_in(key, 103), (SITES, NSEC), SMAX // 2, following + 1)
    whole_at = jnp.roll(full_at, -1)
    kept = jnp.where(sectors == whole_at[:, None], following, kept)
    return (sizes.astype(jnp.int32), kept.astype(jnp.int32))


def draw_sector_sizes(key, part):
    return label_tables(key)[0]


def draw_kept_counts(key, part):
    return label_tables(key)[1]


def touch_ends(values, rng, smallest, largest):
    longest = values.shape.index(max(values.shape))
    spots = []
    for shift in (0, 1):
        where = [jax.random.randint(jax.random.fold_in(rng, axis), (), 0, length) for axis, length in enumerate(values.shape)]
        where[longest] = (where[longest] + shift) % values.shape[longest]
        spots.append(tuple(where))
    return values.at[spots[0]].set(smallest).at[spots[1]].set(largest)


def level_of(own_key, shape, pieces, smallest, top_value):
    level, own = 1.0, jax.random.fold_in(own_key, 6)
    for position, shards_of in pieces:
        draws = jnp.exp(jax.random.uniform(jax.random.fold_in(own, position), (shards_of,), jnp.float32, smallest / len(pieces), top_value / len(pieces)))
        level = level * jnp.repeat(draws, shape[position] // shards_of).reshape([-1 if axis == position else 1 for axis in range(len(shape))])
    return level


def scatter_about(stream_key, extent, scale, most, cuts=(), kind=jnp.bfloat16):
    values = jax.random.normal(stream_key, extent, jnp.float32) * scale
    if len(cuts) > 0:
        values = level_of(stream_key, extent, cuts, -0.22, 0.18) * values
    return jnp.clip(values, min=-most, max=most).astype(kind)


def setup_inputs(seed: int = 0) -> dict:
    key_of = jax.random.split(jax.random.key(seed), 7)
    return {
        "sites": scatter_about(key_of[0], (SITES, 2, NSEC, SMAX, SMAX), SMAX ** -0.5, 0.5, ((0, 32),), jnp.float32),
        "sector_sizes": draw_sector_sizes(jax.random.fold_in(key_of[6], 71), 0),
        "charge_steps": touch_ends(jax.random.randint(key_of[2], (SITES,), 0, 2), jax.random.fold_in(key_of[2], 1), 0, 1).astype(jnp.int32),
        "kept_counts": draw_kept_counts(jax.random.fold_in(key_of[6], 71), 0),
        "gates": jnp.clip(0.4 + 0.800000042 * jax.random.uniform(key_of[4], (SITES, 6), jnp.float32) ** level_of(key_of[4], (SITES, 6), ((0, 32),), -0.2, 0.2), 0.4, 1.2),
        "sketches": scatter_about(key_of[5], (SITES, NSEC, 2 * SMAX, SMAX), (2 * SMAX) ** -0.5, 0.375, ((0, 32),), jnp.float32),
    }


def sector_index(count, shift, extra):
    return ((jnp.arange(count, dtype=jnp.int32) + extra - shift) % count).astype(jnp.int32)

def theta_blocks(left, right, shift, gate):
    count = left.shape[1]
    lower_mid = sector_index(count, shift, 0)
    upper_mid = sector_index(count, shift, 1)

    def product(first, second):
        return jnp.einsum('lam,lmb->lab', first, second, precision=lax.Precision.HIGHEST)
    zero_zero = product(left[0], right[0][lower_mid])
    zero_one = product(left[0], right[1][lower_mid])
    one_zero = product(left[1], right[0][upper_mid])
    one_one = product(left[1], right[1][upper_mid])
    mixed_up = gate[2] * zero_one + gate[3] * one_zero
    mixed_down = gate[4] * zero_one + gate[5] * one_zero
    return (gate[0] * zero_zero, mixed_up, mixed_down, gate[1] * one_one)

def split_sectors(blocks, middle, shift, sketch, kept):
    count = blocks[0].shape[0]
    width = blocks[0].shape[-1]
    top = ((middle + shift) % count).astype(jnp.int32)
    bottom = ((middle + shift - 1) % count).astype(jnp.int32)
    upper = jnp.concatenate([blocks[0][top], blocks[1][top]], axis=2)
    lower = jnp.concatenate([blocks[2][bottom], blocks[3][bottom]], axis=2)
    matrix = jnp.concatenate([upper, lower], axis=1)
    used = (jnp.arange(width, dtype=jnp.int32)[None, :] < kept[:, None]).astype(jnp.float32)
    sample = jnp.einsum('kij,kjs->kis', matrix, sketch * used[:, None, :], precision=lax.Precision.HIGHEST)
    gram = jnp.einsum('kis,kit->kst', sample, sample, precision=lax.Precision.HIGHEST)
    diag_sum = lax.optimization_barrier(jnp.sum(sample * sample, axis=(1, 2)))
    ridge = 0.001 * diag_sum / kept.astype(jnp.float32) + 1e-06
    identity = jnp.eye(width, dtype=jnp.float32)[None]
    gram = gram + identity * ridge[:, None, None] + identity * (1.0 - used)[:, None, :]
    factor = jnp.linalg.cholesky(gram)
    solved = jax.scipy.linalg.solve_triangular(factor, jnp.swapaxes(sample, 1, 2), lower=True)
    basis = jnp.swapaxes(solved, 1, 2)
    reduced = jnp.einsum('kis,kij->ksj', basis, matrix, precision=lax.Precision.HIGHEST)
    return (basis, reduced, jnp.sum(matrix * matrix), jnp.sum(reduced * reduced))

def rebuild(basis, reduced, shift, weight):
    count = basis.shape[0]
    width = basis.shape[2]
    left_new = jnp.stack([basis[sector_index(count, shift, 0), :width], basis[sector_index(count, shift, 1), width:]])
    right_new = jnp.stack([reduced[..., :width], reduced[..., width:]]) / jnp.sqrt(weight)
    return (left_new, right_new)

def bond_update(left, right, shift, gate, sketch, kept):
    blocks = theta_blocks(left, right, shift, gate)
    middle = jnp.arange(left.shape[1], dtype=jnp.int32)
    basis, reduced, total, weight = split_sectors(blocks, middle, shift, sketch, kept)
    left_new, right_new = rebuild(basis, reduced, shift, weight)
    return (left_new, right_new, 1.0 - weight / total, jnp.log(total))

def mask_sites(sites, sizes, steps):
    count = sites.shape[2]
    width = sites.shape[-1]
    following = jnp.roll(sizes, -1, axis=0)
    states = jnp.arange(width, dtype=jnp.int32)
    rows = states[None, None, :] < sizes[:, :, None]
    masks = []
    for phys in range(2):
        target = ((jnp.arange(count, dtype=jnp.int32)[None, :] + phys - steps[:, None]) % count).astype(jnp.int32)
        col_size = jnp.take_along_axis(following, target, axis=1)
        cols = states[None, None, :] < col_size[:, :, None]
        masks.append(rows[:, :, :, None] & cols[:, :, None, :])
    mask = jnp.stack(masks, axis=1)
    return sites * mask.astype(jnp.float32)

def reference(sites, sector_sizes, charge_steps, kept_counts, gates, sketches):
    state = mask_sites(sites, sector_sizes, charge_steps)
    chain = state.shape[0]
    discarded = jnp.zeros((), jnp.float32)
    log_total = jnp.zeros((), jnp.float32)
    for sweep in range(2 * STEPS):
        parity = sweep % 2
        pairs = chain // 2 - parity
        stop = parity + 2 * pairs
        items = (state[parity:stop:2], state[parity + 1:stop + 1:2], charge_steps[parity:stop:2], gates[parity:stop:2], sketches[parity:stop:2], kept_counts[parity:stop:2])

        def one_bond(item):
            return bond_update(item[0], item[1], item[2], item[3], item[4], item[5])
        new_left, new_right, lost, logs = lax.map(one_bond, items)
        state = state.at[parity:stop:2].set(new_left)
        state = state.at[parity + 1:stop + 1:2].set(new_right)
        discarded = discarded + jnp.sum(lost)
        log_total = log_total + jnp.sum(logs)
    return (state, jnp.stack([discarded, log_total]))
```

```python
import functools

import jax
import jax.numpy as jnp
from jax import lax
from jax.experimental import pallas as pl
from jax.experimental.pallas import tpu as pltpu
from jax.sharding import PartitionSpec as P

STEPS = 4
HI = lax.Precision.HIGHEST


def mm(a, b, ca=1, cb=0):
    return lax.dot_general(
        a, b, (((ca,), (cb,)), ((), ())), precision=HI, preferred_element_type=jnp.float32
    )


def inverse_factors(w_ref, z_ref, n, width):
    strip = 32
    lanes = lax.broadcasted_iota(jnp.int32, (1, 8, width), 2)
    subs = lax.broadcasted_iota(jnp.int32, (1, 8, width), 1)
    for b in range(width // strip):
        r0 = b * strip
        groups = strip // 8
        ps = [w_ref[:, r0 + 8 * g : r0 + 8 * g + 8, :] for g in range(groups)]
        if b == 0:
            zs = [
                jnp.broadcast_to((lanes == subs + 8 * g).astype(jnp.float32), ps[0].shape)
                for g in range(groups)
            ]
        else:
            zs = [z_ref[:, r0 + 8 * g : r0 + 8 * g + 8, :] for g in range(groups)]
        for q in range(groups):
            vs = [
                [
                    jnp.broadcast_to(
                        ps[g][:, :, r0 + 8 * q + t : r0 + 8 * q + t + 1], ps[g].shape
                    )
                    if g >= q
                    else None
                    for g in range(groups)
                ]
                for t in range(8)
            ]
            for t in range(8):
                piv = vs[t][q][:, t : t + 1, :]
                inv = lax.rsqrt(piv)
                inv = inv * (1.5 - 0.5 * piv * inv * inv)
                inv2 = inv * inv

                def eliminate(rows):
                    pivot_row = rows[q][:, t : t + 1, :]
                    scaled = pivot_row * inv2
                    out = list(rows)
                    lower = rows[q] - vs[t][q] * scaled
                    out[q] = jnp.where(
                        subs > t, lower, jnp.where(subs == t, rows[q] * inv, rows[q])
                    )
                    for g in range(q + 1, groups):
                        out[g] = rows[g] - vs[t][g] * scaled
                    return out

                ps = eliminate(ps)
                zs = eliminate(zs)
                for t2 in range(t + 1, 8):
                    vs[t2] = eliminate(vs[t2])
        for g in range(groups):
            z_ref[:, r0 + 8 * g : r0 + 8 * g + 8, :] = zs[g]
            w_ref[:, r0 + 8 * g : r0 + 8 * g + 8, :] = ps[g]
        r1 = r0 + strip
        if r1 < width:
            rest = width - r1

            def trail(k, carry, r0=r0, r1=r1, rest=rest, b=b):
                pk = w_ref[k, r0:r1, :]
                zk = z_ref[k, r0:r1, :]
                both = mm(pk, jnp.concatenate([pk, zk], axis=1), 0, 0)[r1:]
                w_ref[k, r1:, :] = w_ref[k, r1:, :] - both[:, :width]
                if b == 0:
                    ri = lax.broadcasted_iota(jnp.int32, (rest, width), 0) + r1
                    ci = lax.broadcasted_iota(jnp.int32, (rest, width), 1)
                    old = (ri == ci).astype(jnp.float32)
                else:
                    old = z_ref[k, r1:, :]
                z_ref[k, r1:, :] = old - both[:, width:]
                return carry

            lax.fori_loop(0, n, trail, 0, unroll=True)


def sweep_kernel(
    n, width, flags, kept, gate,
    own, trav, ex_o, ex_t, sketch, acc,
    own_out, trav_out, ex2, ex3, acc_out,
    xl, xr, mat, smp, w_ref, z_ref, tot, wgt,
):
    full = 2 * n * width
    is_left = flags[0] == 1
    idle = flags[1] == 1

    prev_total = own[full : full + 1, :] + ex_o[2 * width : 2 * width + 1, :]
    prev_weight = own[full + 1 : full + 2, :] + ex_o[2 * width + 1 : 2 * width + 2, :]
    acc_out[...] = acc[...]
    acc_out[0:1, :] = acc[0:1, :] + (1.0 - prev_weight / prev_total)
    acc_out[1:2, :] = acc[1:2, :] + jnp.log(prev_total)
    other_weight = trav[full + 1 : full + 2, :] + ex_t[2 * width + 1 : 2 * width + 2, :]
    scale = 1.0 / jnp.sqrt(jnp.where(is_left, prev_weight, other_weight))

    for p in range(2):
        er = pl.ds(p * width, width)
        eo = ex_o[er, :]
        et = ex_t[er, :]
        xl[p, 0] = jnp.where(is_left, eo, et) * scale
        xr[p, n] = jnp.where(is_left, et, eo)
        for k in range(n):
            hr = pl.ds((p * n + k) * width, width)
            ho = own[hr, :]
            ht = trav[hr, :]
            xl[p, k + 1] = jnp.where(is_left, ho, ht) * scale
            xr[p, k] = jnp.where(is_left, ht, ho)

    def put(k, p, left_block, right_block):
        hr = pl.ds(pl.multiple_of((p * n + k) * width, width), width)
        own_out[hr, :] = jnp.where(is_left, left_block, right_block)
        trav_out[hr, :] = jnp.where(is_left, right_block, left_block)

    def stats(total, weight):
        rows = lax.broadcasted_iota(jnp.int32, (8, width), 0)
        tile = jnp.where(rows == 0, total, jnp.where(rows == 1, weight, 0.0))
        own_out[full : full + 8, :] = tile
        trav_out[full : full + 8, :] = tile
        ex2[2 * width : 2 * width + 8, :] = tile
        ex3[2 * width : 2 * width + 8, :] = tile

    @pl.when(idle)
    def _():
        for k in range(n):
            put(k, 0, xl[0, k + 1], xr[0, k])
            put(k, 1, xl[1, k], xr[1, k + 1])
        half = jnp.full((8, width), 0.5, jnp.float32)
        stats(half, half)

    @pl.when(jnp.logical_not(idle))
    def _():
        g = [gate[i] for i in range(6)]

        def mixes(j, carry):
            s01 = mm(xl[0, j], xr[1, j])
            s10 = mm(xl[1, j], xr[0, j])

            @pl.when(j > 0)
            def _():
                mat[jnp.maximum(j - 1, 0), :width, width:] = g[2] * s01 + g[3] * s10

            @pl.when(j < n)
            def _():
                mat[jnp.minimum(j, n - 1), width:, :width] = g[4] * s01 + g[5] * s10

            return carry

        lax.fori_loop(0, n + 1, mixes, 0, unroll=True)
        tot[...] = jnp.zeros_like(tot)
        wgt[...] = jnp.zeros_like(wgt)
        eye = (
            lax.broadcasted_iota(jnp.int32, (width, width), 0)
            == lax.broadcasted_iota(jnp.int32, (width, width), 1)
        )
        cols = lax.broadcasted_iota(jnp.int32, (1, width), 1)

        def first(k, carry):
            mat[k, :width, :width] = g[0] * mm(xl[0, k + 1], xr[0, k])
            mat[k, width:, width:] = g[1] * mm(xl[1, k], xr[1, k + 1])
            m = mat[k]
            sq = jnp.sum(m * m, axis=0, keepdims=True)
            tot[0:1, :] += sq[:, :width] + sq[:, width:]
            s = mm(m, sketch[k])
            smp[k] = s
            gram = mm(s, s, 0, 0)
            ds = jnp.sum(jnp.sum(s * s, axis=0, keepdims=True), axis=1, keepdims=True)
            kf = kept[k].astype(jnp.float32)
            ridge = 0.001 * ds / kf + 1e-06
            add = ridge + jnp.where(cols < kept[k], 0.0, 1.0)
            w_ref[k] = gram + jnp.where(eye, add, 0.0)
            return carry

        lax.fori_loop(0, n, first, 0, unroll=2)
        inverse_factors(w_ref, z_ref, n, width)

        def second(k, carry):
            basis = mm(smp[k], z_ref[k], 1, 1)
            red = mm(basis, mat[k], 0, 0)
            sq = jnp.sum(red * red, axis=0, keepdims=True)
            wgt[0:1, :] += sq[:, :width] + sq[:, width:]
            put(k, 0, basis[:width], red[:, :width])
            put(k, 1, basis[width:], red[:, width:])
            return carry

        lax.fori_loop(0, n, second, 0, unroll=2)
        t = jnp.sum(tot[0:1, :], axis=1, keepdims=True)
        wt = jnp.sum(wgt[0:1, :], axis=1, keepdims=True)
        stats(jnp.broadcast_to(t, (8, width)), jnp.broadcast_to(wt, (8, width)))

    for p in range(2):
        er = pl.ds(p * width, width)
        low = pl.ds(p * n * width, width)
        high = pl.ds((p * n + n - 1) * width, width)
        ex2[er, :] = jnp.where(is_left, trav_out[high, :], trav_out[low, :])
        ex3[er, :] = jnp.where(is_left, own_out[low, :], own_out[high, :])


def run_sweep(n, width, flags, kept, gate, own, trav, ex_o, ex_t, sketch, acc):
    f32 = jnp.float32
    big = jax.ShapeDtypeStruct((2 * n * width + 8, width), f32)
    small = jax.ShapeDtypeStruct((2 * width + 8, width), f32)
    smem = pl.BlockSpec(memory_space=pltpu.SMEM)
    vmem = pl.BlockSpec(memory_space=pltpu.VMEM)
    return pl.pallas_call(
        functools.partial(sweep_kernel, n, width),
        out_shape=(big, big, small, small, jax.ShapeDtypeStruct((8, width), f32)),
        in_specs=[smem] * 3 + [vmem] * 6,
        out_specs=(vmem,) * 5,
        scratch_shapes=[
            pltpu.VMEM((2, n + 1, width, width), f32),
            pltpu.VMEM((2, n + 1, width, width), f32),
            pltpu.VMEM((n, 2 * width, 2 * width), f32),
            pltpu.VMEM((n, 2 * width, width), f32),
            pltpu.VMEM((n, width, width), f32),
            pltpu.VMEM((n, width, width), f32),
            pltpu.VMEM((8, width), f32),
            pltpu.VMEM((8, width), f32),
        ],
        compiler_params=pltpu.CompilerParams(vmem_limit_bytes=40 * 1024 * 1024),
    )(flags, kept, gate, own, trav, ex_o, ex_t, sketch, acc)


def body(sites, sector_sizes, charge_steps, kept_counts, gates, sketches):
    f32 = jnp.float32
    chain = lax.axis_size("site")
    pos = lax.axis_index("site")
    count, width = sites.shape[2], sites.shape[-1]
    n = count // 2
    par = pos % 2
    odd = par == 1

    table = jnp.concatenate(
        [
            sector_sizes.astype(f32),
            kept_counts.astype(f32),
            charge_steps.astype(f32)[:, None],
            gates,
        ],
        axis=1,
    )
    table = lax.all_gather(table, "site", axis=0, tiled=True)
    steps = table[:, 2 * count].astype(jnp.int32)
    before = jnp.sum(jnp.where(jnp.arange(chain) < pos, steps, 0))
    step = charge_steps[0]
    prev = (pos + chain - 1) % chain
    following = lax.dynamic_index_in_dim(table, (pos + 1) % chain, 0, keepdims=False)[:count]
    prev_row = lax.dynamic_index_in_dim(table, prev, 0, keepdims=False)

    secs = jnp.arange(count, dtype=jnp.int32)
    mine = (secs[:n] + par * n)
    theirs = (secs[:n] + (1 - par) * n)
    order = jnp.concatenate(
        [
            mine,
            jnp.where(odd, 0, count - 1)[None].astype(jnp.int32),
            theirs,
            jnp.where(odd, n, n - 1)[None].astype(jnp.int32),
        ]
    )
    states = jnp.arange(width, dtype=jnp.int32)
    rows = states[None, :] < sector_sizes[0][:, None]
    pieces = []
    for p in range(2):
        label = (order - before - jnp.where(odd, p, 0)) % count
        target = (label + p - step) % count
        kr = rows[label]
        kc = states[None, :].astype(f32) < following[target][:, None]
        mask = kr[:, :, None] & kc[:, None, :]
        pieces.append(jnp.where(mask, sites[0, p][label], 0.0))
    both = jnp.stack(pieces)
    stat = jnp.where((jnp.arange(8) < 2)[:, None], 0.5, 0.0) * jnp.ones((1, width), f32)

    def flat(blocks):
        return jnp.concatenate([blocks.reshape(-1, width), stat], axis=0)

    own = flat(both[:, :n])
    ex_o = flat(both[:, n])
    even_pairs = [(i, i ^ 1) for i in range(chain)]
    odd_pairs = [
        (i, (i + 1) % chain if i % 2 == 1 else (i - 1) % chain) for i in range(chain)
    ]

    def perm(value, pairs):
        return lax.ppermute(value, "site", pairs)

    trav = perm(flat(both[:, n + 1 : 2 * n + 1]), even_pairs)
    ex_t = perm(flat(both[:, 2 * n + 1]), even_pairs)

    after = before + step
    own_sk = sketches[0][(mine - after) % count]
    send_sk = sketches[0][(theirs - after) % count]
    got_sk = perm(send_sk, [(i, (i + 1) % chain) for i in range(chain)])
    own_kept = kept_counts[0][(mine - after) % count]
    prev_kept = prev_row[count : 2 * count].astype(jnp.int32)[(mine - before) % count]
    own_sk = own_sk * (states[None, :] < own_kept[:, None]).astype(f32)[:, None, :]
    got_sk = got_sk * (states[None, :] < prev_kept[:, None]).astype(f32)[:, None, :]
    own_gate = gates[0]
    prev_gate = prev_row[2 * count + 1 :]
    sk, kp, gt, fl, moves, near, far = [], [], [], [], [], [], []
    for sweep in range(2):
        left = par == sweep
        sk.append(jnp.where(left, own_sk, got_sk))
        kp.append(jnp.where(left, own_kept, prev_kept))
        gt.append(jnp.where(left, own_gate, prev_gate))
        idle = (sweep == 1) & ((pos == 0) | (pos == chain - 1))
        fl.append(jnp.stack([left.astype(jnp.int32), idle.astype(jnp.int32)]))
        moves.append([(i, (i + (2 if i % 2 == sweep else -2)) % chain) for i in range(chain)])
        near.append(odd_pairs if sweep else even_pairs)
        far.append(even_pairs if sweep else odd_pairs)

    def call(sweep, own, trav, ex_o, ex_t, acc):
        return run_sweep(
            n, width, fl[sweep], kp[sweep], gt[sweep], own, trav, ex_o, ex_t, sk[sweep], acc
        )

    def one_sweep(sweep, carry):
        own, trav, ex2, ex3, acc = call(sweep, *carry)
        return (
            own, perm(trav, moves[sweep]), perm(ex2, near[sweep]), perm(ex3, far[sweep]), acc,
        )

    carry = one_sweep(0, (own, trav, ex_o, ex_t, jnp.zeros((8, width), f32)))

    def pair(index, carry):
        return one_sweep(0, one_sweep(1, carry))

    carry = lax.fori_loop(0, STEPS - 1, pair, carry)
    own, trav, _, _, acc = call(1, *carry)
    got = perm(trav, odd_pairs)
    full = 2 * n * width
    total = own[full, 0] + got[full, 0]
    weight = own[full + 1, 0] + got[full + 1, 0]
    sums = jnp.stack([acc[0, 0] + (1.0 - weight / total), acc[1, 0] + jnp.log(total)])
    sums = 0.5 * lax.psum(sums, "site")
    scale = jnp.where(odd, 1.0, 1.0 / jnp.sqrt(weight))
    halves = jnp.stack(
        [own[:full].reshape(2, n, width, width), got[:full].reshape(2, n, width, width)], axis=1
    ).reshape(2, count, width, width)
    out = []
    for p in range(2):
        charge = (secs + before + jnp.where(odd, p, 0)) % count
        out.append(halves[p][(charge + par * n) % count])
    return ((jnp.stack(out) * scale)[None], sums)


def solution(mesh):
    placed = (
        P("site", None, None, None, None),
        P("site", None),
        P("site"),
        P("site", None),
        P("site", None),
        P("site", None, None, None),
    )
    return jax.shard_map(
        body,
        mesh=mesh,
        in_specs=placed,
        out_specs=(P("site", None, None, None, None), P()),
        check_vma=False,
    )
```

```python
import functools

import jax
import jax.numpy as jnp
from jax import lax
from jax.experimental import pallas as pl
from jax.experimental.pallas import tpu as pltpu
from jax.sharding import PartitionSpec as P

STEPS = 4
HI = lax.Precision.HIGHEST


def mm(a, b, ca=1, cb=0):
    return lax.dot_general(
        a, b, (((ca,), (cb,)), ((), ())), precision=HI, preferred_element_type=jnp.float32
    )


def inverse_factors(w_ref, z_ref, n, width):
    strip = 32
    lanes = lax.broadcasted_iota(jnp.int32, (1, 8, width), 2)
    subs = lax.broadcasted_iota(jnp.int32, (1, 8, width), 1)
    for b in range(width // strip):
        r0 = b * strip
        groups = strip // 8
        ps = [w_ref[:, r0 + 8 * g : r0 + 8 * g + 8, :] for g in range(groups)]
        if b == 0:
            zs = [
                jnp.broadcast_to((lanes == subs + 8 * g).astype(jnp.float32), ps[0].shape)
                for g in range(groups)
            ]
        else:
            zs = [z_ref[:, r0 + 8 * g : r0 + 8 * g + 8, :] for g in range(groups)]
        for q in range(groups):
            vs = [
                [
                    jnp.broadcast_to(
                        ps[g][:, :, r0 + 8 * q + t : r0 + 8 * q + t + 1], ps[g].shape
                    )
                    if g >= q
                    else None
                    for g in range(groups)
                ]
                for t in range(8)
            ]
            for t in range(8):
                piv = vs[t][q][:, t : t + 1, :]
                inv = lax.rsqrt(piv)
                inv = inv * (1.5 - 0.5 * piv * inv * inv)
                inv2 = inv * inv

                def eliminate(rows):
                    pivot_row = rows[q][:, t : t + 1, :]
                    scaled = pivot_row * inv2
                    out = list(rows)
                    lower = rows[q] - vs[t][q] * scaled
                    out[q] = jnp.where(
                        subs > t, lower, jnp.where(subs == t, rows[q] * inv, rows[q])
                    )
                    for g in range(q + 1, groups):
                        out[g] = rows[g] - vs[t][g] * scaled
                    return out

                ps = eliminate(ps)
                zs = eliminate(zs)
                for t2 in range(t + 1, 8):
                    vs[t2] = eliminate(vs[t2])
        for g in range(groups):
            z_ref[:, r0 + 8 * g : r0 + 8 * g + 8, :] = zs[g]
            w_ref[:, r0 + 8 * g : r0 + 8 * g + 8, :] = ps[g]
        r1 = r0 + strip
        if r1 < width:
            rest = width - r1

            def trail(k, carry, r0=r0, r1=r1, rest=rest, b=b):
                pk = w_ref[k, r0:r1, :]
                zk = z_ref[k, r0:r1, :]
                both = mm(pk, jnp.concatenate([pk, zk], axis=1), 0, 0)[r1:]
                w_ref[k, r1:, :] = w_ref[k, r1:, :] - both[:, :width]
                if b == 0:
                    ri = lax.broadcasted_iota(jnp.int32, (rest, width), 0) + r1
                    ci = lax.broadcasted_iota(jnp.int32, (rest, width), 1)
                    old = (ri == ci).astype(jnp.float32)
                else:
                    old = z_ref[k, r1:, :]
                z_ref[k, r1:, :] = old - both[:, width:]
                return carry

            lax.fori_loop(0, n, trail, 0, unroll=True)


def sweep_kernel(
    n, width, sweep, kept, gate,
    own, trav, ex_o, ex_t, own_sk, got_sk,
    own_out, trav_out, ex2, ex3,
    xl, xr, mat, smp, w_ref, z_ref, tot, wgt,
):
    full = 2 * n * width
    me = lax.axis_index("site")
    chain = lax.axis_size("site")
    is_left = lax.rem(me, 2) == sweep
    idle = ((me == 0) | (me == chain - 1)) if sweep == 1 else (me < 0)
    which = jnp.where(is_left, 0, 1)

    prev_total = own[full : full + 1, :] + ex_o[2 * width : 2 * width + 1, :]
    prev_weight = own[full + 1 : full + 2, :] + ex_o[2 * width + 1 : 2 * width + 2, :]
    lost = own[full + 2 : full + 3, :] + (1.0 - prev_weight / prev_total)
    logs = own[full + 3 : full + 4, :] + jnp.log(prev_total)
    other_weight = trav[full + 1 : full + 2, :] + ex_t[2 * width + 1 : 2 * width + 2, :]
    scale = 1.0 / jnp.sqrt(jnp.where(is_left, prev_weight, other_weight))

    for p in range(2):
        er = pl.ds(p * width, width)
        eo = ex_o[er, :]
        et = ex_t[er, :]
        xl[p, 0] = jnp.where(is_left, eo, et) * scale
        xr[p, n] = jnp.where(is_left, et, eo)
        for k in range(n):
            hr = pl.ds((p * n + k) * width, width)
            ho = own[hr, :]
            ht = trav[hr, :]
            xl[p, k + 1] = jnp.where(is_left, ho, ht) * scale
            xr[p, k] = jnp.where(is_left, ht, ho)

    def put(k, p, left_block, right_block):
        hr = pl.ds(pl.multiple_of((p * n + k) * width, width), width)
        own_out[hr, :] = jnp.where(is_left, left_block, right_block)
        trav_out[hr, :] = jnp.where(is_left, right_block, left_block)

    def stats(total, weight):
        rows = lax.broadcasted_iota(jnp.int32, (8, width), 0)
        tile = jnp.where(rows == 0, total, jnp.where(rows == 1, weight, 0.0))
        tile = jnp.where(rows == 2, lost, jnp.where(rows == 3, logs, tile))
        own_out[full : full + 8, :] = tile
        trav_out[full : full + 8, :] = tile
        ex2[2 * width : 2 * width + 8, :] = tile
        ex3[2 * width : 2 * width + 8, :] = tile

    @pl.when(idle)
    def _():
        for k in range(n):
            put(k, 0, xl[0, k + 1], xr[0, k])
            put(k, 1, xl[1, k], xr[1, k + 1])
        half = jnp.full((8, width), 0.5, jnp.float32)
        stats(half, half)

    @pl.when(jnp.logical_not(idle))
    def _():
        g = [gate[which, i] for i in range(6)]

        def mixes(j, carry):
            s01 = mm(xl[0, j], xr[1, j])
            s10 = mm(xl[1, j], xr[0, j])

            @pl.when(j > 0)
            def _():
                mat[jnp.maximum(j - 1, 0), :width, width:] = g[2] * s01 + g[3] * s10

            @pl.when(j < n)
            def _():
                mat[jnp.minimum(j, n - 1), width:, :width] = g[4] * s01 + g[5] * s10

            return carry

        lax.fori_loop(0, n + 1, mixes, 0)
        tot[...] = jnp.zeros_like(tot)
        wgt[...] = jnp.zeros_like(wgt)
        eye = (
            lax.broadcasted_iota(jnp.int32, (width, width), 0)
            == lax.broadcasted_iota(jnp.int32, (width, width), 1)
        )
        cols = lax.broadcasted_iota(jnp.int32, (1, width), 1)

        def first(k, carry):
            mat[k, :width, :width] = g[0] * mm(xl[0, k + 1], xr[0, k])
            mat[k, width:, width:] = g[1] * mm(xl[1, k], xr[1, k + 1])
            m = mat[k]
            sq = jnp.sum(m * m, axis=0, keepdims=True)
            tot[0:1, :] += sq[:, :width] + sq[:, width:]
            used = cols < kept[which, k]
            s = mm(m, jnp.where(used, jnp.where(is_left, own_sk[k], got_sk[k]), 0.0))
            smp[k] = s
            gram = mm(s, s, 0, 0)
            ds = jnp.sum(jnp.sum(s * s, axis=0, keepdims=True), axis=1, keepdims=True)
            kf = kept[which, k].astype(jnp.float32)
            ridge = 0.001 * ds / kf + 1e-06
            add = ridge + jnp.where(used, 0.0, 1.0)
            w_ref[k] = gram + jnp.where(eye, add, 0.0)
            return carry

        lax.fori_loop(0, n, first, 0, unroll=1)
        inverse_factors(w_ref, z_ref, n, width)

        def second(k, carry):
            basis = mm(smp[k], z_ref[k], 1, 1)
            red = mm(basis, mat[k], 0, 0)
            sq = jnp.sum(red * red, axis=0, keepdims=True)
            wgt[0:1, :] += sq[:, :width] + sq[:, width:]
            put(k, 0, basis[:width], red[:, :width])
            put(k, 1, basis[width:], red[:, width:])
            return carry

        lax.fori_loop(0, n, second, 0, unroll=1)
        t = jnp.sum(tot[0:1, :], axis=1, keepdims=True)
        wt = jnp.sum(wgt[0:1, :], axis=1, keepdims=True)
        stats(jnp.broadcast_to(t, (8, width)), jnp.broadcast_to(wt, (8, width)))

    for p in range(2):
        er = pl.ds(p * width, width)
        low = pl.ds(p * n * width, width)
        high = pl.ds((p * n + n - 1) * width, width)
        ex2[er, :] = jnp.where(is_left, trav_out[high, :], trav_out[low, :])
        ex3[er, :] = jnp.where(is_left, own_out[low, :], own_out[high, :])


def run_sweep(n, width, sweep, kept, gate, own, trav, ex_o, ex_t, own_sk, got_sk):
    f32 = jnp.float32
    big = jax.ShapeDtypeStruct((2 * n * width + 8, width), f32)
    small = jax.ShapeDtypeStruct((2 * width + 8, width), f32)
    smem = pl.BlockSpec(memory_space=pltpu.SMEM)
    vmem = pl.BlockSpec(memory_space=pltpu.VMEM)
    return pl.pallas_call(
        functools.partial(sweep_kernel, n, width, sweep),
        out_shape=(big, big, small, small),
        in_specs=[smem] * 2 + [vmem] * 6,
        out_specs=(vmem,) * 4,
        scratch_shapes=[
            pltpu.VMEM((2, n + 1, width, width), f32),
            pltpu.VMEM((2, n + 1, width, width), f32),
            pltpu.VMEM((n, 2 * width, 2 * width), f32),
            pltpu.VMEM((n, 2 * width, width), f32),
            pltpu.VMEM((n, width, width), f32),
            pltpu.VMEM((n, width, width), f32),
            pltpu.VMEM((8, width), f32),
            pltpu.VMEM((8, width), f32),
        ],
        compiler_params=pltpu.CompilerParams(vmem_limit_bytes=40 * 1024 * 1024),
    )(kept, gate, own, trav, ex_o, ex_t, own_sk, got_sk)


MESH = pl.DeviceIdType.MESH


def even_partner(me, chain):
    return me + 1 - 2 * lax.rem(me, 2)


def odd_partner(me, chain):
    return lax.rem(me - 1 + 2 * lax.rem(me, 2) + chain, chain)


def ahead(by):
    return lambda me, chain: lax.rem(me + by + chain, chain)


def travel(sweep, back):
    def to(me, chain):
        by = 2 - 4 * lax.rem(me + sweep, 2)
        return lax.rem(me + (-by if back else by) + chain, chain)

    return to


def exchange_kernel(routes, *refs):
    me, chain = lax.axis_index("site"), lax.axis_size("site")
    count = len(routes)
    ins, outs, (send, recv) = refs[:count], refs[count : 2 * count], refs[2 * count :]
    barrier = pltpu.get_barrier_semaphore()
    for _, source in routes:
        pl.semaphore_signal(
            barrier, inc=1, device_id=(source(me, chain),), device_id_type=MESH
        )
    pl.semaphore_wait(barrier, count)
    copies = []
    for i, (to, _) in enumerate(routes):
        copy = pltpu.make_async_remote_copy(
            src_ref=ins[i], dst_ref=outs[i], send_sem=send.at[i], recv_sem=recv.at[i],
            device_id=(to(me, chain),), device_id_type=MESH,
        )
        copy.start()
        copies.append(copy)
    for copy in copies:
        copy.wait()


def exchange(cid, routes, *values):
    anywhere = pl.BlockSpec(memory_space=pl.ANY)
    count = len(routes)
    return pl.pallas_call(
        functools.partial(exchange_kernel, routes),
        out_shape=tuple(jax.ShapeDtypeStruct(v.shape, v.dtype) for v in values),
        in_specs=[anywhere] * count,
        out_specs=(anywhere,) * count,
        scratch_shapes=[pltpu.SemaphoreType.DMA((count,)), pltpu.SemaphoreType.DMA((count,))],
        compiler_params=pltpu.CompilerParams(collective_id=cid, has_side_effects=True),
    )(*values)


def spread_kernel(chain, routed, *refs):
    if routed:
        tile, value, out, value_out, send, recv, one_send, one_recv = refs
    else:
        tile, out, send, recv = refs
    me = lax.axis_index("site")
    barrier = pltpu.get_barrier_semaphore()

    def greet(off, carry):
        pl.semaphore_signal(
            barrier, inc=1, device_id=(lax.rem(me + off, chain),), device_id_type=MESH
        )
        return carry

    lax.fori_loop(1, chain, greet, 0)
    pl.semaphore_wait(barrier, chain - 1)
    if routed:
        one = pltpu.make_async_remote_copy(
            src_ref=value, dst_ref=value_out, send_sem=one_send, recv_sem=one_recv,
            device_id=(odd_partner(me, chain),), device_id_type=MESH,
        )
        one.start()

    def copy(off):
        return pltpu.make_async_remote_copy(
            src_ref=tile, dst_ref=out.at[me], send_sem=send.at[off], recv_sem=recv.at[off],
            device_id=(lax.rem(me + off, chain),), device_id_type=MESH,
        )

    def begin(off, carry):
        copy(off).start()
        return carry

    def finish(off, carry):
        copy(off).wait()
        return carry

    lax.fori_loop(1, chain, begin, 0)
    out[me] = tile[...]
    lax.fori_loop(1, chain, finish, 0)
    if routed:
        one.wait()


def spread(cid, chain, tile, value=None):
    vmem = pl.BlockSpec(memory_space=pltpu.VMEM)
    anywhere = pl.BlockSpec(memory_space=pl.ANY)
    routed = value is not None
    shapes = [jax.ShapeDtypeStruct((chain,) + tile.shape, tile.dtype)]
    sems = [pltpu.SemaphoreType.DMA((chain,)), pltpu.SemaphoreType.DMA((chain,))]
    ins, specs, args = [vmem], [vmem], [tile]
    if routed:
        shapes.append(jax.ShapeDtypeStruct(value.shape, value.dtype))
        sems += [pltpu.SemaphoreType.DMA, pltpu.SemaphoreType.DMA]
        ins, specs, args = [vmem, anywhere], [vmem, anywhere], [tile, value]
    return pl.pallas_call(
        functools.partial(spread_kernel, chain, routed),
        out_shape=tuple(shapes),
        in_specs=ins,
        out_specs=tuple(specs),
        scratch_shapes=sems,
        compiler_params=pltpu.CompilerParams(collective_id=cid, has_side_effects=True),
    )(*args)


def body(sites, sector_sizes, charge_steps, kept_counts, gates, sketches):
    f32 = jnp.float32
    chain = lax.axis_size("site")
    pos = lax.axis_index("site")
    count, width = sites.shape[2], sites.shape[-1]
    n = count // 2
    par = pos % 2
    odd = par == 1

    table = jnp.concatenate(
        [
            sector_sizes.astype(f32),
            kept_counts.astype(f32),
            charge_steps.astype(f32)[:, None],
            gates,
        ],
        axis=1,
    )
    used = table.shape[1]
    tile = jnp.pad(table, ((0, 7), (0, width - used)))
    table = spread(1, chain, tile)[0][:, 0, :used]
    steps = table[:, 2 * count].astype(jnp.int32)
    before = jnp.sum(jnp.where(jnp.arange(chain) < pos, steps, 0))
    step = charge_steps[0]
    prev = (pos + chain - 1) % chain
    following = lax.dynamic_index_in_dim(table, (pos + 1) % chain, 0, keepdims=False)[:count]
    prev_row = lax.dynamic_index_in_dim(table, prev, 0, keepdims=False)

    secs = jnp.arange(count, dtype=jnp.int32)
    mine = (secs[:n] + par * n)
    theirs = (secs[:n] + (1 - par) * n)
    order = jnp.concatenate(
        [
            mine,
            jnp.where(odd, 0, count - 1)[None].astype(jnp.int32),
            theirs,
            jnp.where(odd, n, n - 1)[None].astype(jnp.int32),
        ]
    )
    states = jnp.arange(width, dtype=jnp.int32)
    rows = states[None, :] < sector_sizes[0][:, None]
    pieces = []
    for p in range(2):
        label = (order - before - jnp.where(odd, p, 0)) % count
        target = (label + p - step) % count
        kr = rows[label]
        kc = states[None, :].astype(f32) < following[target][:, None]
        mask = kr[:, :, None] & kc[:, None, :]
        pieces.append(jnp.where(mask, sites[0, p][label], 0.0))
    both = jnp.stack(pieces)
    stat = jnp.where((jnp.arange(8) < 2)[:, None], 0.5, 0.0) * jnp.ones((1, width), f32)

    def flat(blocks):
        return jnp.concatenate([blocks.reshape(-1, width), stat], axis=0)

    own = flat(both[:, :n])
    ex_o = flat(both[:, n])
    after = before + step
    own_sk = sketches[0][(mine - after) % count]
    send_sk = sketches[0][(theirs - after) % count]
    trav, ex_t, got_sk = exchange(
        2,
        ((even_partner, even_partner), (even_partner, even_partner), (ahead(1), ahead(-1))),
        flat(both[:, n + 1 : 2 * n + 1]),
        flat(both[:, 2 * n + 1]),
        send_sk,
    )
    own_kept = kept_counts[0][(mine - after) % count]
    prev_kept = prev_row[count : 2 * count].astype(jnp.int32)[(mine - before) % count]
    kept = jnp.stack([own_kept, prev_kept])
    gate = jnp.stack([gates[0], prev_row[2 * count + 1 : used]])
    partners = (even_partner, odd_partner)

    def call(sweep, own, trav, ex_o, ex_t):
        return run_sweep(n, width, sweep, kept, gate, own, trav, ex_o, ex_t, own_sk, got_sk)

    def one_sweep(sweep, carry):
        own, trav, ex2, ex3 = call(sweep, *carry)
        near, far = partners[sweep], partners[1 - sweep]
        routes = ((travel(sweep, False), travel(sweep, True)), (near, near), (far, far))
        return (own,) + tuple(exchange(3 + sweep, routes, trav, ex2, ex3))

    carry = one_sweep(0, (own, trav, ex_o, ex_t))

    def pair(index, carry):
        return one_sweep(0, one_sweep(1, carry))

    carry = lax.fori_loop(0, STEPS - 1, pair, carry)
    own, trav, _, _ = call(1, *carry)
    full = 2 * n * width
    tiles, got = spread(5, chain, own[full:], trav)
    weight = own[full + 1, 0] + got[full + 1, 0]
    stats = tiles[:, :4, 0]
    bonds = jnp.sum(jnp.roll(stats[:, :2], -1, axis=0).reshape(chain // 2, 2, 2), axis=1)
    sums = jnp.stack(
        [
            0.5 * jnp.sum(stats[:, 2]) + jnp.sum(1.0 - bonds[:, 1] / bonds[:, 0]),
            0.5 * jnp.sum(stats[:, 3]) + jnp.sum(jnp.log(bonds[:, 0])),
        ]
    )
    scale = jnp.where(odd, 1.0, 1.0 / jnp.sqrt(weight))
    halves = jnp.stack(
        [own[:full].reshape(2, n, width, width), got[:full].reshape(2, n, width, width)], axis=1
    ).reshape(2, count, width, width)
    out = []
    for p in range(2):
        charge = (secs + before + jnp.where(odd, p, 0)) % count
        out.append(halves[p][(charge + par * n) % count])
    return ((jnp.stack(out) * scale)[None], sums)


def solution(mesh):
    placed = (
        P("site", None, None, None, None),
        P("site", None),
        P("site"),
        P("site", None),
        P("site", None),
        P("site", None, None, None),
    )
    return jax.shard_map(
        body,
        mesh=mesh,
        in_specs=placed,
        out_specs=(P("site", None, None, None, None), P()),
        check_vma=False,
    )
```

```python
import functools

import jax
import jax.numpy as jnp
from jax import lax
from jax.experimental import pallas as pl
from jax.experimental.pallas import tpu as pltpu
from jax.sharding import PartitionSpec as P

STEPS = 4
HI = lax.Precision.HIGHEST


def mm(a, b, ca=1, cb=0):
    return lax.dot_general(
        a, b, (((ca,), (cb,)), ((), ())), precision=HI, preferred_element_type=jnp.float32
    )


def inverse_factors(w_ref, z_ref, n, width):
    strip = 32
    lanes = lax.broadcasted_iota(jnp.int32, (1, 8, width), 2)
    subs = lax.broadcasted_iota(jnp.int32, (1, 8, width), 1)
    for b in range(width // strip):
        r0 = b * strip
        groups = strip // 8
        ps = [w_ref[:, r0 + 8 * g : r0 + 8 * g + 8, :] for g in range(groups)]
        if b == 0:
            zs = [
                jnp.broadcast_to((lanes == subs + 8 * g).astype(jnp.float32), ps[0].shape)
                for g in range(groups)
            ]
        else:
            zs = [z_ref[:, r0 + 8 * g : r0 + 8 * g + 8, :] for g in range(groups)]
        for q in range(groups):
            vs = [
                [
                    jnp.broadcast_to(
                        ps[g][:, :, r0 + 8 * q + t : r0 + 8 * q + t + 1], ps[g].shape
                    )
                    if g >= q
                    else None
                    for g in range(groups)
                ]
                for t in range(8)
            ]
            for t in range(8):
                piv = vs[t][q][:, t : t + 1, :]
                inv = lax.rsqrt(piv)
                inv = inv * (1.5 - 0.5 * piv * inv * inv)
                inv2 = inv * inv

                def eliminate(rows):
                    pivot_row = rows[q][:, t : t + 1, :]
                    scaled = pivot_row * inv2
                    out = list(rows)
                    lower = rows[q] - vs[t][q] * scaled
                    out[q] = jnp.where(
                        subs > t, lower, jnp.where(subs == t, rows[q] * inv, rows[q])
                    )
                    for g in range(q + 1, groups):
                        out[g] = rows[g] - vs[t][g] * scaled
                    return out

                ps = eliminate(ps)
                zs = eliminate(zs)
                for t2 in range(t + 1, 8):
                    vs[t2] = eliminate(vs[t2])
        for g in range(groups):
            z_ref[:, r0 + 8 * g : r0 + 8 * g + 8, :] = zs[g]
            w_ref[:, r0 + 8 * g : r0 + 8 * g + 8, :] = ps[g]
        r1 = r0 + strip
        if r1 < width:
            rest = width - r1

            def trail(k, carry, r0=r0, r1=r1, rest=rest, b=b):
                pk = w_ref[k, r0:r1, :]
                zk = z_ref[k, r0:r1, :]
                both = mm(pk, jnp.concatenate([pk, zk], axis=1), 0, 0)[r1:]
                w_ref[k, r1:, :] = w_ref[k, r1:, :] - both[:, :width]
                if b == 0:
                    ri = lax.broadcasted_iota(jnp.int32, (rest, width), 0) + r1
                    ci = lax.broadcasted_iota(jnp.int32, (rest, width), 1)
                    old = (ri == ci).astype(jnp.float32)
                else:
                    old = z_ref[k, r1:, :]
                z_ref[k, r1:, :] = old - both[:, width:]
                return carry

            lax.fori_loop(0, n, trail, 0, unroll=True)


def sweep_kernel(
    n, width, sweep, kept, gate,
    own, trav, ex_o, ex_t, own_sk, got_sk,
    own_out, trav_out, ex2, ex3,
    xl, xr, mat, smp, w_ref, z_ref, tot, wgt,
):
    full = 2 * n * width
    me = lax.axis_index("site")
    chain = lax.axis_size("site")
    is_left = lax.rem(me, 2) == sweep
    idle = ((me == 0) | (me == chain - 1)) if sweep == 1 else (me < 0)
    which = jnp.where(is_left, 0, 1)

    prev_total = own[full : full + 1, :] + ex_o[2 * width : 2 * width + 1, :]
    prev_weight = own[full + 1 : full + 2, :] + ex_o[2 * width + 1 : 2 * width + 2, :]
    lost = own[full + 2 : full + 3, :] + (1.0 - prev_weight / prev_total)
    logs = own[full + 3 : full + 4, :] + jnp.log(prev_total)
    other_weight = trav[full + 1 : full + 2, :] + ex_t[2 * width + 1 : 2 * width + 2, :]
    scale = 1.0 / jnp.sqrt(jnp.where(is_left, prev_weight, other_weight))

    for p in range(2):
        er = pl.ds(p * width, width)
        eo = ex_o[er, :]
        et = ex_t[er, :]
        xl[p, 0] = jnp.where(is_left, eo, et) * scale
        xr[p, n] = jnp.where(is_left, et, eo)
        for k in range(n):
            hr = pl.ds((p * n + k) * width, width)
            ho = own[hr, :]
            ht = trav[hr, :]
            xl[p, k + 1] = jnp.where(is_left, ho, ht) * scale
            xr[p, k] = jnp.where(is_left, ht, ho)

    def put(k, p, left_block, right_block):
        hr = pl.ds(pl.multiple_of((p * n + k) * width, width), width)
        own_out[hr, :] = jnp.where(is_left, left_block, right_block)
        trav_out[hr, :] = jnp.where(is_left, right_block, left_block)

    def stats(total, weight):
        rows = lax.broadcasted_iota(jnp.int32, (8, width), 0)
        tile = jnp.where(rows == 0, total, jnp.where(rows == 1, weight, 0.0))
        tile = jnp.where(rows == 2, lost, jnp.where(rows == 3, logs, tile))
        own_out[full : full + 8, :] = tile
        trav_out[full : full + 8, :] = tile
        ex2[2 * width : 2 * width + 8, :] = tile
        ex3[2 * width : 2 * width + 8, :] = tile

    @pl.when(idle)
    def _():
        for k in range(n):
            put(k, 0, xl[0, k + 1], xr[0, k])
            put(k, 1, xl[1, k], xr[1, k + 1])
        half = jnp.full((8, width), 0.5, jnp.float32)
        stats(half, half)

    @pl.when(jnp.logical_not(idle))
    def _():
        g = [gate[which, i] for i in range(6)]

        def mixes(j, carry):
            s01 = mm(xl[0, j], xr[1, j])
            s10 = mm(xl[1, j], xr[0, j])

            @pl.when(j > 0)
            def _():
                mat[jnp.maximum(j - 1, 0), :width, width:] = g[2] * s01 + g[3] * s10

            @pl.when(j < n)
            def _():
                mat[jnp.minimum(j, n - 1), width:, :width] = g[4] * s01 + g[5] * s10

            return carry

        lax.fori_loop(0, n + 1, mixes, 0, unroll=True)
        tot[...] = jnp.zeros_like(tot)
        wgt[...] = jnp.zeros_like(wgt)
        eye = (
            lax.broadcasted_iota(jnp.int32, (width, width), 0)
            == lax.broadcasted_iota(jnp.int32, (width, width), 1)
        )
        cols = lax.broadcasted_iota(jnp.int32, (1, width), 1)

        def first(k, carry):
            mat[k, :width, :width] = g[0] * mm(xl[0, k + 1], xr[0, k])
            mat[k, width:, width:] = g[1] * mm(xl[1, k], xr[1, k + 1])
            m = mat[k]
            sq = jnp.sum(m * m, axis=0, keepdims=True)
            tot[0:1, :] += sq[:, :width] + sq[:, width:]
            used = cols < kept[which, k]
            s = mm(m, jnp.where(used, jnp.where(is_left, own_sk[k], got_sk[k]), 0.0))
            smp[k] = s
            gram = mm(s, s, 0, 0)
            ds = jnp.sum(jnp.sum(s * s, axis=0, keepdims=True), axis=1, keepdims=True)
            kf = kept[which, k].astype(jnp.float32)
            ridge = 0.001 * ds / kf + 1e-06
            add = ridge + jnp.where(used, 0.0, 1.0)
            w_ref[k] = gram + jnp.where(eye, add, 0.0)
            return carry

        lax.fori_loop(0, n, first, 0, unroll=2)
        inverse_factors(w_ref, z_ref, n, width)

        def second(k, carry):
            basis = mm(smp[k], z_ref[k], 1, 1)
            red = mm(basis, mat[k], 0, 0)
            sq = jnp.sum(red * red, axis=0, keepdims=True)
            wgt[0:1, :] += sq[:, :width] + sq[:, width:]
            put(k, 0, basis[:width], red[:, :width])
            put(k, 1, basis[width:], red[:, width:])
            return carry

        lax.fori_loop(0, n, second, 0, unroll=2)
        t = jnp.sum(tot[0:1, :], axis=1, keepdims=True)
        wt = jnp.sum(wgt[0:1, :], axis=1, keepdims=True)
        stats(jnp.broadcast_to(t, (8, width)), jnp.broadcast_to(wt, (8, width)))

    for p in range(2):
        er = pl.ds(p * width, width)
        low = pl.ds(p * n * width, width)
        high = pl.ds((p * n + n - 1) * width, width)
        ex2[er, :] = jnp.where(is_left, trav_out[high, :], trav_out[low, :])
        ex3[er, :] = jnp.where(is_left, own_out[low, :], own_out[high, :])


def run_sweep(n, width, sweep, kept, gate, own, trav, ex_o, ex_t, own_sk, got_sk):
    f32 = jnp.float32
    big = jax.ShapeDtypeStruct((2 * n * width + 8, width), f32)
    small = jax.ShapeDtypeStruct((2 * width + 8, width), f32)
    smem = pl.BlockSpec(memory_space=pltpu.SMEM)
    vmem = pl.BlockSpec(memory_space=pltpu.VMEM)
    return pl.pallas_call(
        functools.partial(sweep_kernel, n, width, sweep),
        out_shape=(big, big, small, small),
        in_specs=[smem] * 2 + [vmem] * 6,
        out_specs=(vmem,) * 4,
        scratch_shapes=[
            pltpu.VMEM((2, n + 1, width, width), f32),
            pltpu.VMEM((2, n + 1, width, width), f32),
            pltpu.VMEM((n, 2 * width, 2 * width), f32),
            pltpu.VMEM((n, 2 * width, width), f32),
            pltpu.VMEM((n, width, width), f32),
            pltpu.VMEM((n, width, width), f32),
            pltpu.VMEM((8, width), f32),
            pltpu.VMEM((8, width), f32),
        ],
        compiler_params=pltpu.CompilerParams(vmem_limit_bytes=40 * 1024 * 1024),
    )(kept, gate, own, trav, ex_o, ex_t, own_sk, got_sk)


MESH = pl.DeviceIdType.MESH


def even_partner(me, chain):
    return me + 1 - 2 * lax.rem(me, 2)


def odd_partner(me, chain):
    return lax.rem(me - 1 + 2 * lax.rem(me, 2) + chain, chain)


def ahead(by):
    return lambda me, chain: lax.rem(me + by + chain, chain)


def travel(sweep, back):
    def to(me, chain):
        by = 2 - 4 * lax.rem(me + sweep, 2)
        return lax.rem(me + (-by if back else by) + chain, chain)

    return to


def exchange_kernel(routes, *refs):
    me, chain = lax.axis_index("site"), lax.axis_size("site")
    count = len(routes)
    ins, outs, (send, recv) = refs[:count], refs[count : 2 * count], refs[2 * count :]
    barrier = pltpu.get_barrier_semaphore()
    for _, source in routes:
        pl.semaphore_signal(
            barrier, inc=1, device_id=(source(me, chain),), device_id_type=MESH
        )
    pl.semaphore_wait(barrier, count)
    copies = []
    for i, (to, _) in enumerate(routes):
        copy = pltpu.make_async_remote_copy(
            src_ref=ins[i], dst_ref=outs[i], send_sem=send.at[i], recv_sem=recv.at[i],
            device_id=(to(me, chain),), device_id_type=MESH,
        )
        copy.start()
        copies.append(copy)
    for copy in copies:
        copy.wait()


def exchange(cid, routes, *values):
    anywhere = pl.BlockSpec(memory_space=pl.ANY)
    count = len(routes)
    return pl.pallas_call(
        functools.partial(exchange_kernel, routes),
        out_shape=tuple(jax.ShapeDtypeStruct(v.shape, v.dtype) for v in values),
        in_specs=[anywhere] * count,
        out_specs=(anywhere,) * count,
        scratch_shapes=[pltpu.SemaphoreType.DMA((count,)), pltpu.SemaphoreType.DMA((count,))],
        compiler_params=pltpu.CompilerParams(collective_id=cid, has_side_effects=True),
    )(*values)


def spread_kernel(chain, routed, *refs):
    if routed:
        tile, value, out, value_out, send, recv, one_send, one_recv = refs
    else:
        tile, out, send, recv = refs
    me = lax.axis_index("site")
    barrier = pltpu.get_barrier_semaphore()

    def greet(off, carry):
        pl.semaphore_signal(
            barrier, inc=1, device_id=(lax.rem(me + off, chain),), device_id_type=MESH
        )
        return carry

    lax.fori_loop(1, chain, greet, 0)
    pl.semaphore_wait(barrier, chain - 1)
    if routed:
        one = pltpu.make_async_remote_copy(
            src_ref=value, dst_ref=value_out, send_sem=one_send, recv_sem=one_recv,
            device_id=(odd_partner(me, chain),), device_id_type=MESH,
        )
        one.start()

    def copy(off):
        return pltpu.make_async_remote_copy(
            src_ref=tile, dst_ref=out.at[me], send_sem=send.at[off], recv_sem=recv.at[off],
            device_id=(lax.rem(me + off, chain),), device_id_type=MESH,
        )

    def begin(off, carry):
        copy(off).start()
        return carry

    def finish(off, carry):
        copy(off).wait()
        return carry

    lax.fori_loop(1, chain, begin, 0)
    out[me] = tile[...]
    lax.fori_loop(1, chain, finish, 0)
    if routed:
        one.wait()


def spread(cid, chain, tile, value=None):
    vmem = pl.BlockSpec(memory_space=pltpu.VMEM)
    anywhere = pl.BlockSpec(memory_space=pl.ANY)
    routed = value is not None
    shapes = [jax.ShapeDtypeStruct((chain,) + tile.shape, tile.dtype)]
    sems = [pltpu.SemaphoreType.DMA((chain,)), pltpu.SemaphoreType.DMA((chain,))]
    ins, specs, args = [vmem], [vmem], [tile]
    if routed:
        shapes.append(jax.ShapeDtypeStruct(value.shape, value.dtype))
        sems += [pltpu.SemaphoreType.DMA, pltpu.SemaphoreType.DMA]
        ins, specs, args = [vmem, anywhere], [vmem, anywhere], [tile, value]
    return pl.pallas_call(
        functools.partial(spread_kernel, chain, routed),
        out_shape=tuple(shapes),
        in_specs=ins,
        out_specs=tuple(specs),
        scratch_shapes=sems,
        compiler_params=pltpu.CompilerParams(collective_id=cid, has_side_effects=True),
    )(*args)


def body(sites, sector_sizes, charge_steps, kept_counts, gates, sketches):
    f32 = jnp.float32
    chain = lax.axis_size("site")
    pos = lax.axis_index("site")
    count, width = sites.shape[2], sites.shape[-1]
    n = count // 2
    par = pos % 2
    odd = par == 1

    table = jnp.concatenate(
        [
            sector_sizes.astype(f32),
            kept_counts.astype(f32),
            charge_steps.astype(f32)[:, None],
            gates,
        ],
        axis=1,
    )
    used = table.shape[1]
    tile = jnp.pad(table, ((0, 7), (0, width - used)))
    table = spread(1, chain, tile)[0][:, 0, :used]
    steps = table[:, 2 * count].astype(jnp.int32)
    before = jnp.sum(jnp.where(jnp.arange(chain) < pos, steps, 0))
    step = charge_steps[0]
    prev = (pos + chain - 1) % chain
    following = lax.dynamic_index_in_dim(table, (pos + 1) % chain, 0, keepdims=False)[:count]
    prev_row = lax.dynamic_index_in_dim(table, prev, 0, keepdims=False)

    secs = jnp.arange(count, dtype=jnp.int32)
    mine = (secs[:n] + par * n)
    theirs = (secs[:n] + (1 - par) * n)
    order = jnp.concatenate(
        [
            mine,
            jnp.where(odd, 0, count - 1)[None].astype(jnp.int32),
            theirs,
            jnp.where(odd, n, n - 1)[None].astype(jnp.int32),
        ]
    )
    states = jnp.arange(width, dtype=jnp.int32)
    rows = states[None, :] < sector_sizes[0][:, None]
    pieces = []
    for p in range(2):
        label = (order - before - jnp.where(odd, p, 0)) % count
        target = (label + p - step) % count
        kr = rows[label]
        kc = states[None, :].astype(f32) < following[target][:, None]
        mask = kr[:, :, None] & kc[:, None, :]
        pieces.append(jnp.where(mask, sites[0, p][label], 0.0))
    both = jnp.stack(pieces)
    stat = jnp.where((jnp.arange(8) < 2)[:, None], 0.5, 0.0) * jnp.ones((1, width), f32)

    def flat(blocks):
        return jnp.concatenate([blocks.reshape(-1, width), stat], axis=0)

    own = flat(both[:, :n])
    ex_o = flat(both[:, n])
    after = before + step
    own_sk = sketches[0][(mine - after) % count]
    send_sk = sketches[0][(theirs - after) % count]
    trav, ex_t, got_sk = exchange(
        2,
        ((even_partner, even_partner), (even_partner, even_partner), (ahead(1), ahead(-1))),
        flat(both[:, n + 1 : 2 * n + 1]),
        flat(both[:, 2 * n + 1]),
        send_sk,
    )
    own_kept = kept_counts[0][(mine - after) % count]
    prev_kept = prev_row[count : 2 * count].astype(jnp.int32)[(mine - before) % count]
    kept = jnp.stack([own_kept, prev_kept])
    gate = jnp.stack([gates[0], prev_row[2 * count + 1 : used]])
    partners = (even_partner, odd_partner)

    def call(sweep, own, trav, ex_o, ex_t):
        return run_sweep(n, width, sweep, kept, gate, own, trav, ex_o, ex_t, own_sk, got_sk)

    def one_sweep(sweep, carry):
        own, trav, ex2, ex3 = call(sweep, *carry)
        near, far = partners[sweep], partners[1 - sweep]
        routes = ((travel(sweep, False), travel(sweep, True)), (near, near), (far, far))
        return (own,) + tuple(exchange(3 + sweep, routes, trav, ex2, ex3))

    carry = one_sweep(0, (own, trav, ex_o, ex_t))

    def pair(index, carry):
        return one_sweep(0, one_sweep(1, carry))

    carry = lax.fori_loop(0, STEPS - 1, pair, carry)
    own, trav, _, _ = call(1, *carry)
    full = 2 * n * width
    tiles, got = spread(5, chain, own[full:], trav)
    weight = own[full + 1, 0] + got[full + 1, 0]
    stats = tiles[:, :4, 0]
    bonds = jnp.sum(jnp.roll(stats[:, :2], -1, axis=0).reshape(chain // 2, 2, 2), axis=1)
    sums = jnp.stack(
        [
            0.5 * jnp.sum(stats[:, 2]) + jnp.sum(1.0 - bonds[:, 1] / bonds[:, 0]),
            0.5 * jnp.sum(stats[:, 3]) + jnp.sum(jnp.log(bonds[:, 0])),
        ]
    )
    scale = jnp.where(odd, 1.0, 1.0 / jnp.sqrt(weight))
    halves = jnp.stack(
        [own[:full].reshape(2, n, width, width), got[:full].reshape(2, n, width, width)], axis=1
    ).reshape(2, count, width, width)
    out = []
    for p in range(2):
        charge = (secs + before + jnp.where(odd, p, 0)) % count
        out.append(halves[p][(charge + par * n) % count])
    return ((jnp.stack(out) * scale)[None], sums)


def solution(mesh):
    placed = (
        P("site", None, None, None, None),
        P("site", None),
        P("site"),
        P("site", None),
        P("site", None),
        P("site", None, None, None),
    )
    return jax.shard_map(
        body,
        mesh=mesh,
        in_specs=placed,
        out_specs=(P("site", None, None, None, None), P()),
        check_vma=False,
    )
```

```python
import functools

import jax
import jax.numpy as jnp
from jax import lax
from jax.experimental import pallas as pl
from jax.experimental.pallas import tpu as pltpu
from jax.sharding import PartitionSpec as P

STEPS = 4
HI = lax.Precision.HIGHEST


def mm(a, b, ca=1, cb=0):
    return lax.dot_general(
        a, b, (((ca,), (cb,)), ((), ())), precision=HI, preferred_element_type=jnp.float32
    )


def inverse_factors(w_ref, z_ref, n, width):
    strip = 32
    lanes = lax.broadcasted_iota(jnp.int32, (1, 8, width), 2)
    subs = lax.broadcasted_iota(jnp.int32, (1, 8, width), 1)
    for b in range(width // strip):
        r0 = b * strip
        groups = strip // 8
        ps = [w_ref[:, r0 + 8 * g : r0 + 8 * g + 8, :] for g in range(groups)]
        if b == 0:
            zs = [
                jnp.broadcast_to((lanes == subs + 8 * g).astype(jnp.float32), ps[0].shape)
                for g in range(groups)
            ]
        else:
            zs = [z_ref[:, r0 + 8 * g : r0 + 8 * g + 8, :] for g in range(groups)]
        for q in range(groups):
            vs = [
                [
                    jnp.broadcast_to(
                        ps[g][:, :, r0 + 8 * q + t : r0 + 8 * q + t + 1], ps[g].shape
                    )
                    if g >= q
                    else None
                    for g in range(groups)
                ]
                for t in range(8)
            ]
            for t in range(8):
                piv = vs[t][q][:, t : t + 1, :]
                inv = lax.rsqrt(piv)
                inv = inv * (1.5 - 0.5 * piv * inv * inv)
                inv2 = inv * inv

                def eliminate(rows):
                    pivot_row = rows[q][:, t : t + 1, :]
                    scaled = pivot_row * inv2
                    out = list(rows)
                    lower = rows[q] - vs[t][q] * scaled
                    out[q] = jnp.where(
                        subs > t, lower, jnp.where(subs == t, rows[q] * inv, rows[q])
                    )
                    for g in range(q + 1, groups):
                        out[g] = rows[g] - vs[t][g] * scaled
                    return out

                ps = eliminate(ps)
                zs = eliminate(zs)
                for t2 in range(t + 1, 8):
                    vs[t2] = eliminate(vs[t2])
        for g in range(groups):
            z_ref[:, r0 + 8 * g : r0 + 8 * g + 8, :] = zs[g]
            w_ref[:, r0 + 8 * g : r0 + 8 * g + 8, :] = ps[g]
        r1 = r0 + strip
        if r1 < width:
            rest = width - r1

            def trail(k, carry, r0=r0, r1=r1, rest=rest, b=b):
                pk = w_ref[k, r0:r1, :]
                zk = z_ref[k, r0:r1, :]
                both = mm(pk, jnp.concatenate([pk, zk], axis=1), 0, 0)[r1:]
                w_ref[k, r1:, :] = w_ref[k, r1:, :] - both[:, :width]
                if b == 0:
                    ri = lax.broadcasted_iota(jnp.int32, (rest, width), 0) + r1
                    ci = lax.broadcasted_iota(jnp.int32, (rest, width), 1)
                    old = (ri == ci).astype(jnp.float32)
                else:
                    old = z_ref[k, r1:, :]
                z_ref[k, r1:, :] = old - both[:, width:]
                return carry

            lax.fori_loop(0, n, trail, 0, unroll=True)


def sweep_kernel(
    n, width, sweep, unroll, kept, gate,
    own, trav, ex_o, ex_t, own_sk, got_sk,
    own_out, trav_out, ex2, ex3,
    xl, xr, mat, smp, w_ref, z_ref, tot, wgt,
):
    full = 2 * n * width
    me = lax.axis_index("site")
    chain = lax.axis_size("site")
    is_left = lax.rem(me, 2) == sweep
    idle = ((me == 0) | (me == chain - 1)) if sweep == 1 else (me < 0)
    which = jnp.where(is_left, 0, 1)

    prev_total = own[full : full + 1, :] + ex_o[2 * width : 2 * width + 1, :]
    prev_weight = own[full + 1 : full + 2, :] + ex_o[2 * width + 1 : 2 * width + 2, :]
    lost = own[full + 2 : full + 3, :] + (1.0 - prev_weight / prev_total)
    logs = own[full + 3 : full + 4, :] + jnp.log(prev_total)
    other_weight = trav[full + 1 : full + 2, :] + ex_t[2 * width + 1 : 2 * width + 2, :]
    scale = 1.0 / jnp.sqrt(jnp.where(is_left, prev_weight, other_weight))

    for p in range(2):
        er = pl.ds(p * width, width)
        eo = ex_o[er, :]
        et = ex_t[er, :]
        xl[p, 0] = jnp.where(is_left, eo, et) * scale
        xr[p, n] = jnp.where(is_left, et, eo)
        for k in range(n):
            hr = pl.ds((p * n + k) * width, width)
            ho = own[hr, :]
            ht = trav[hr, :]
            xl[p, k + 1] = jnp.where(is_left, ho, ht) * scale
            xr[p, k] = jnp.where(is_left, ht, ho)

    def put(k, p, left_block, right_block):
        hr = pl.ds(pl.multiple_of((p * n + k) * width, width), width)
        own_out[hr, :] = jnp.where(is_left, left_block, right_block)
        trav_out[hr, :] = jnp.where(is_left, right_block, left_block)

    def stats(total, weight):
        rows = lax.broadcasted_iota(jnp.int32, (8, width), 0)
        tile = jnp.where(rows == 0, total, jnp.where(rows == 1, weight, 0.0))
        tile = jnp.where(rows == 2, lost, jnp.where(rows == 3, logs, tile))
        own_out[full : full + 8, :] = tile
        trav_out[full : full + 8, :] = tile
        ex2[2 * width : 2 * width + 8, :] = tile
        ex3[2 * width : 2 * width + 8, :] = tile

    @pl.when(idle)
    def _():
        for k in range(n):
            put(k, 0, xl[0, k + 1], xr[0, k])
            put(k, 1, xl[1, k], xr[1, k + 1])
        half = jnp.full((8, width), 0.5, jnp.float32)
        stats(half, half)

    @pl.when(jnp.logical_not(idle))
    def _():
        g = [gate[which, i] for i in range(6)]

        def mixes(j, carry):
            s01 = mm(xl[0, j], xr[1, j])
            s10 = mm(xl[1, j], xr[0, j])

            @pl.when(j > 0)
            def _():
                mat[jnp.maximum(j - 1, 0), :width, width:] = g[2] * s01 + g[3] * s10

            @pl.when(j < n)
            def _():
                mat[jnp.minimum(j, n - 1), width:, :width] = g[4] * s01 + g[5] * s10

            return carry

        lax.fori_loop(0, n + 1, mixes, 0, unroll=n + 1 if unroll > 1 else 1)
        tot[...] = jnp.zeros_like(tot)
        wgt[...] = jnp.zeros_like(wgt)
        eye = (
            lax.broadcasted_iota(jnp.int32, (width, width), 0)
            == lax.broadcasted_iota(jnp.int32, (width, width), 1)
        )
        cols = lax.broadcasted_iota(jnp.int32, (1, width), 1)

        def first(k, carry):
            mat[k, :width, :width] = g[0] * mm(xl[0, k + 1], xr[0, k])
            mat[k, width:, width:] = g[1] * mm(xl[1, k], xr[1, k + 1])
            m = mat[k]
            sq = jnp.sum(m * m, axis=0, keepdims=True)
            tot[0:1, :] += sq[:, :width] + sq[:, width:]
            used = cols < kept[which, k]
            s = mm(m, jnp.where(used, jnp.where(is_left, own_sk[k], got_sk[k]), 0.0))
            smp[k] = s
            gram = mm(s, s, 0, 0)
            ds = jnp.sum(jnp.sum(s * s, axis=0, keepdims=True), axis=1, keepdims=True)
            kf = kept[which, k].astype(jnp.float32)
            ridge = 0.001 * ds / kf + 1e-06
            add = ridge + jnp.where(used, 0.0, 1.0)
            w_ref[k] = gram + jnp.where(eye, add, 0.0)
            return carry

        lax.fori_loop(0, n, first, 0, unroll=unroll)
        inverse_factors(w_ref, z_ref, n, width)

        def second(k, carry):
            basis = mm(smp[k], z_ref[k], 1, 1)
            red = mm(basis, mat[k], 0, 0)
            sq = jnp.sum(red * red, axis=0, keepdims=True)
            wgt[0:1, :] += sq[:, :width] + sq[:, width:]
            put(k, 0, basis[:width], red[:, :width])
            put(k, 1, basis[width:], red[:, width:])
            return carry

        lax.fori_loop(0, n, second, 0, unroll=unroll)
        t = jnp.sum(tot[0:1, :], axis=1, keepdims=True)
        wt = jnp.sum(wgt[0:1, :], axis=1, keepdims=True)
        stats(jnp.broadcast_to(t, (8, width)), jnp.broadcast_to(wt, (8, width)))

    for p in range(2):
        er = pl.ds(p * width, width)
        low = pl.ds(p * n * width, width)
        high = pl.ds((p * n + n - 1) * width, width)
        ex2[er, :] = jnp.where(is_left, trav_out[high, :], trav_out[low, :])
        ex3[er, :] = jnp.where(is_left, own_out[low, :], own_out[high, :])


def run_sweep(n, width, sweep, unroll, kept, gate, own, trav, ex_o, ex_t, own_sk, got_sk):
    f32 = jnp.float32
    big = jax.ShapeDtypeStruct((2 * n * width + 8, width), f32)
    small = jax.ShapeDtypeStruct((2 * width + 8, width), f32)
    smem = pl.BlockSpec(memory_space=pltpu.SMEM)
    vmem = pl.BlockSpec(memory_space=pltpu.VMEM)
    return pl.pallas_call(
        functools.partial(sweep_kernel, n, width, sweep, unroll),
        out_shape=(big, big, small, small),
        in_specs=[smem] * 2 + [vmem] * 6,
        out_specs=(vmem,) * 4,
        scratch_shapes=[
            pltpu.VMEM((2, n + 1, width, width), f32),
            pltpu.VMEM((2, n + 1, width, width), f32),
            pltpu.VMEM((n, 2 * width, 2 * width), f32),
            pltpu.VMEM((n, 2 * width, width), f32),
            pltpu.VMEM((n, width, width), f32),
            pltpu.VMEM((n, width, width), f32),
            pltpu.VMEM((8, width), f32),
            pltpu.VMEM((8, width), f32),
        ],
        compiler_params=pltpu.CompilerParams(vmem_limit_bytes=40 * 1024 * 1024),
    )(kept, gate, own, trav, ex_o, ex_t, own_sk, got_sk)


MESH = pl.DeviceIdType.MESH


def even_partner(me, chain):
    return me + 1 - 2 * lax.rem(me, 2)


def odd_partner(me, chain):
    return lax.rem(me - 1 + 2 * lax.rem(me, 2) + chain, chain)


def ahead(by):
    return lambda me, chain: lax.rem(me + by + chain, chain)


def travel(sweep, back):
    def to(me, chain):
        by = 2 - 4 * lax.rem(me + sweep, 2)
        return lax.rem(me + (-by if back else by) + chain, chain)

    return to


def exchange_kernel(routes, *refs):
    me, chain = lax.axis_index("site"), lax.axis_size("site")
    count = len(routes)
    ins, outs, (send, recv) = refs[:count], refs[count : 2 * count], refs[2 * count :]
    barrier = pltpu.get_barrier_semaphore()
    for _, source in routes:
        pl.semaphore_signal(
            barrier, inc=1, device_id=(source(me, chain),), device_id_type=MESH
        )
    pl.semaphore_wait(barrier, count)
    copies = []
    for i, (to, _) in enumerate(routes):
        copy = pltpu.make_async_remote_copy(
            src_ref=ins[i], dst_ref=outs[i], send_sem=send.at[i], recv_sem=recv.at[i],
            device_id=(to(me, chain),), device_id_type=MESH,
        )
        copy.start()
        copies.append(copy)
    for copy in copies:
        copy.wait()


def exchange(cid, routes, *values):
    anywhere = pl.BlockSpec(memory_space=pl.ANY)
    count = len(routes)
    return pl.pallas_call(
        functools.partial(exchange_kernel, routes),
        out_shape=tuple(jax.ShapeDtypeStruct(v.shape, v.dtype) for v in values),
        in_specs=[anywhere] * count,
        out_specs=(anywhere,) * count,
        scratch_shapes=[pltpu.SemaphoreType.DMA((count,)), pltpu.SemaphoreType.DMA((count,))],
        compiler_params=pltpu.CompilerParams(collective_id=cid, has_side_effects=True),
    )(*values)


def spread_kernel(chain, routed, *refs):
    if routed:
        tile, value, out, value_out, send, recv, one_send, one_recv = refs
    else:
        tile, out, send, recv = refs
    me = lax.axis_index("site")
    barrier = pltpu.get_barrier_semaphore()

    def greet(off, carry):
        pl.semaphore_signal(
            barrier, inc=1, device_id=(lax.rem(me + off, chain),), device_id_type=MESH
        )
        return carry

    lax.fori_loop(1, chain, greet, 0)
    pl.semaphore_wait(barrier, chain - 1)
    if routed:
        one = pltpu.make_async_remote_copy(
            src_ref=value, dst_ref=value_out, send_sem=one_send, recv_sem=one_recv,
            device_id=(odd_partner(me, chain),), device_id_type=MESH,
        )
        one.start()

    def copy(off):
        return pltpu.make_async_remote_copy(
            src_ref=tile, dst_ref=out.at[me], send_sem=send.at[off], recv_sem=recv.at[off],
            device_id=(lax.rem(me + off, chain),), device_id_type=MESH,
        )

    def begin(off, carry):
        copy(off).start()
        return carry

    def finish(off, carry):
        copy(off).wait()
        return carry

    lax.fori_loop(1, chain, begin, 0)
    out[me] = tile[...]
    lax.fori_loop(1, chain, finish, 0)
    if routed:
        one.wait()


def spread(cid, chain, tile, value=None):
    vmem = pl.BlockSpec(memory_space=pltpu.VMEM)
    anywhere = pl.BlockSpec(memory_space=pl.ANY)
    routed = value is not None
    shapes = [jax.ShapeDtypeStruct((chain,) + tile.shape, tile.dtype)]
    sems = [pltpu.SemaphoreType.DMA((chain,)), pltpu.SemaphoreType.DMA((chain,))]
    ins, specs, args = [vmem], [vmem], [tile]
    if routed:
        shapes.append(jax.ShapeDtypeStruct(value.shape, value.dtype))
        sems += [pltpu.SemaphoreType.DMA, pltpu.SemaphoreType.DMA]
        ins, specs, args = [vmem, anywhere], [vmem, anywhere], [tile, value]
    return pl.pallas_call(
        functools.partial(spread_kernel, chain, routed),
        out_shape=tuple(shapes),
        in_specs=ins,
        out_specs=tuple(specs),
        scratch_shapes=sems,
        compiler_params=pltpu.CompilerParams(collective_id=cid, has_side_effects=True),
    )(*args)


def body(sites, sector_sizes, charge_steps, kept_counts, gates, sketches):
    f32 = jnp.float32
    chain = lax.axis_size("site")
    pos = lax.axis_index("site")
    count, width = sites.shape[2], sites.shape[-1]
    n = count // 2
    par = pos % 2
    odd = par == 1

    table = jnp.concatenate(
        [
            sector_sizes.astype(f32),
            kept_counts.astype(f32),
            charge_steps.astype(f32)[:, None],
            gates,
        ],
        axis=1,
    )
    used = table.shape[1]
    tile = jnp.pad(table, ((0, 7), (0, width - used)))
    table = spread(1, chain, tile)[0][:, 0, :used]
    steps = table[:, 2 * count].astype(jnp.int32)
    before = jnp.sum(jnp.where(jnp.arange(chain) < pos, steps, 0))
    step = charge_steps[0]
    prev = (pos + chain - 1) % chain
    following = lax.dynamic_index_in_dim(table, (pos + 1) % chain, 0, keepdims=False)[:count]
    prev_row = lax.dynamic_index_in_dim(table, prev, 0, keepdims=False)

    secs = jnp.arange(count, dtype=jnp.int32)
    mine = (secs[:n] + par * n)
    theirs = (secs[:n] + (1 - par) * n)
    order = jnp.concatenate(
        [
            mine,
            jnp.where(odd, 0, count - 1)[None].astype(jnp.int32),
            theirs,
            jnp.where(odd, n, n - 1)[None].astype(jnp.int32),
        ]
    )
    states = jnp.arange(width, dtype=jnp.int32)
    rows = states[None, :] < sector_sizes[0][:, None]
    pieces = []
    for p in range(2):
        label = (order - before - jnp.where(odd, p, 0)) % count
        target = (label + p - step) % count
        kr = rows[label]
        kc = states[None, :].astype(f32) < following[target][:, None]
        mask = kr[:, :, None] & kc[:, None, :]
        pieces.append(jnp.where(mask, sites[0, p][label], 0.0))
    both = jnp.stack(pieces)
    stat = jnp.where((jnp.arange(8) < 2)[:, None], 0.5, 0.0) * jnp.ones((1, width), f32)

    def flat(blocks):
        return jnp.concatenate([blocks.reshape(-1, width), stat], axis=0)

    own = flat(both[:, :n])
    ex_o = flat(both[:, n])
    after = before + step
    own_sk = sketches[0][(mine - after) % count]
    send_sk = sketches[0][(theirs - after) % count]
    trav, ex_t, got_sk = exchange(
        2,
        ((even_partner, even_partner), (even_partner, even_partner), (ahead(1), ahead(-1))),
        flat(both[:, n + 1 : 2 * n + 1]),
        flat(both[:, 2 * n + 1]),
        send_sk,
    )
    own_kept = kept_counts[0][(mine - after) % count]
    prev_kept = prev_row[count : 2 * count].astype(jnp.int32)[(mine - before) % count]
    kept = jnp.stack([own_kept, prev_kept])
    gate = jnp.stack([gates[0], prev_row[2 * count + 1 : used]])
    partners = (even_partner, odd_partner)

    def call(sweep, unroll, own, trav, ex_o, ex_t):
        return run_sweep(n, width, sweep, unroll, kept, gate, own, trav, ex_o, ex_t, own_sk, got_sk)

    def one_sweep(sweep, unroll, carry):
        own, trav, ex2, ex3 = call(sweep, unroll, *carry)
        near, far = partners[sweep], partners[1 - sweep]
        routes = ((travel(sweep, False), travel(sweep, True)), (near, near), (far, far))
        return (own,) + tuple(exchange(3 + sweep, routes, trav, ex2, ex3))

    carry = one_sweep(0, 1, (own, trav, ex_o, ex_t))

    def pair(index, carry):
        return one_sweep(0, 2, one_sweep(1, 2, carry))

    carry = lax.fori_loop(0, STEPS - 1, pair, carry)
    own, trav, _, _ = call(1, 1, *carry)
    full = 2 * n * width
    tiles, got = spread(5, chain, own[full:], trav)
    weight = own[full + 1, 0] + got[full + 1, 0]
    stats = tiles[:, :4, 0]
    bonds = jnp.sum(jnp.roll(stats[:, :2], -1, axis=0).reshape(chain // 2, 2, 2), axis=1)
    sums = jnp.stack(
        [
            0.5 * jnp.sum(stats[:, 2]) + jnp.sum(1.0 - bonds[:, 1] / bonds[:, 0]),
            0.5 * jnp.sum(stats[:, 3]) + jnp.sum(jnp.log(bonds[:, 0])),
        ]
    )
    scale = jnp.where(odd, 1.0, 1.0 / jnp.sqrt(weight))
    halves = jnp.stack(
        [own[:full].reshape(2, n, width, width), got[:full].reshape(2, n, width, width)], axis=1
    ).reshape(2, count, width, width)
    out = []
    for p in range(2):
        charge = (secs + before + jnp.where(odd, p, 0)) % count
        out.append(halves[p][(charge + par * n) % count])
    return ((jnp.stack(out) * scale)[None], sums)


def solution(mesh):
    placed = (
        P("site", None, None, None, None),
        P("site", None),
        P("site"),
        P("site", None),
        P("site", None),
        P("site", None, None, None),
    )
    return jax.shard_map(
        body,
        mesh=mesh,
        in_specs=placed,
        out_specs=(P("site", None, None, None, None), P()),
        check_vma=False,
    )
```
